32 devices in a mesh: groups: 2 (over y), section: 16 (over z, x, core).
Axes of the slice: x: 2, y: 2, z: 4, core: 2. Of those that a mesh axis runs over, the one named last changes fastest.
Arguments:
- held: bfloat16 [16, 128, 4096], P('section', 'groups'), parts along dimension 1, may hold values from 0 to 2
- tile_values: bfloat16 [4608, 128, 128], P('section'), may hold values from -0.25 to 0.25
- tile_rows: int32 [4608], P('section'), may hold values from 0 to 255
- tile_cols: int32 [4608], P('section'), may hold values from 0 to 31
- tile_count: int32 [16], P('section'), may hold values from 1 to 288, as said below
- bias: float32 [65536], P('section'), may hold values from -0.5 to -0.2
Outputs:
- settled: bfloat16 [16, 128, 4096], P('section', 'groups'), parts along dimension 1
The draws below stay inside these ranges and needn't reach their ends.
There are 2 independent parts, one for each index of `groups`. The reference program is written for one: setup_inputs(seed, part) draws one part's arguments, and reference() takes and returns one part's arrays. A program takes and returns all parts, laid end to end along the dimension named above; an argument that names none is the same for every part. Nothing has to cross between parts.
Inputs may be any that keep to these rules, and one draw needn't show every extreme that they name: `tile_count`: slots at or after a list's count are ignored; in every draw some list has all 288 slots live. `tile_rows`: pairs of tile row and tile column may repeat within a list; repeated tiles add.
All inputs are finite; a program needn't handle non-finite values.
Results may differ from the reference program's by a relative error of at most 0.0053.
Values may be sent and summed in bfloat16 or wider, within the bound.
No kernel may reach another device: no remote copies, remote signals or barrier semaphores. Data moves between devices by JAX's collectives and lax.ppermute only.
A program may use at most 64 MiB of HBM per device.

```python
import jax
import jax.numpy as jnp
from jax import lax

TILE = 128
NTILES = 256
SPLIT = 8
CAP = 288
TICKS = 2
BATCH = 64
NEURONS = 32768
SLAB = 4096
COLT = 32
LAYERS = 2


def draw_tile_count(key, part):
    total_lists = LAYERS * SPLIT
    key_first = jax.random.fold_in(key, 11)
    key_second = jax.random.fold_in(key, 23)
    bottom = max(1, CAP // 10)
    ceiling = CAP * 7 // 10 + 1
    counts = jax.random.randint(key_first, (total_lists,), bottom, ceiling, dtype=jnp.int32)
    chosen = jax.random.randint(key_second, (), 0, total_lists, dtype=jnp.int32)
    return jnp.where(jnp.arange(total_lists, dtype=jnp.int32) == chosen, CAP, counts).astype(jnp.int32)


def plant(values, rng, low, largest):
    index_at = [jax.random.randint(jax.random.fold_in(rng, axis), (), 0, length) for axis, length in enumerate(values.shape)]
    longest = values.shape.index(max(values.shape))
    next_to = index_at[:longest] + [(index_at[longest] + 1) % values.shape[longest]] + index_at[longest + 1:]
    return values.at[tuple(index_at)].set(low).at[tuple(next_to)].set(largest)


def block_scale(key, extent, split, low, high):
    def one(axis_at, parts):
        heights = jax.random.uniform(jax.random.fold_in(jax.random.fold_in(key, 6), axis_at), (parts,), jnp.float32, low / len(split), high / len(split))
        return jnp.repeat(jnp.exp(heights), extent[axis_at] // parts).reshape((-1,) + (1,) * (len(extent) - axis_at - 1))

    loudness = one(*split[0])
    for cut in split[1:]:
        loudness = loudness * one(*cut)
    return loudness


def gaussian(key, extent, spread, limit, cuts=(), kind=jnp.bfloat16):
    gain = block_scale(key, extent, cuts, -0.22, 0.18) if cuts else 1.0
    result = jax.random.normal(key, extent, jnp.float32) * spread * gain
    return jnp.minimum(jnp.maximum(result, -limit), limit).astype(kind)


def setup_inputs(seed: int = 0, part: int = 0) -> dict:
    key_list = jax.random.split(jax.random.key(seed), 7)
    part_keys = jax.random.split(jax.random.fold_in(key_list[6], part), 7)
    held = jnp.clip(2.0 * jax.random.uniform(part_keys[0], (LAYERS * SPLIT, BATCH, SLAB), jnp.float32) ** block_scale(part_keys[0], (LAYERS * SPLIT, BATCH, SLAB), ((0, 16),), -0.2, 0.2), 0.0, 2.0).astype(jnp.bfloat16)
    tile_values = gaussian(key_list[1], (LAYERS * SPLIT * CAP, TILE, TILE), (max(NTILES * TILE // 64, 4 * TILE)) ** -0.5, 0.25, ((0, 16),))
    tile_rows = plant(jax.random.randint(key_list[2], (LAYERS * SPLIT * CAP,), 0, NTILES), jax.random.fold_in(key_list[2], 1), 0, NTILES - 1).astype(jnp.int32)
    tile_cols = plant(jax.random.randint(key_list[3], (LAYERS * SPLIT * CAP,), 0, COLT), jax.random.fold_in(key_list[3], 1), 0, COLT - 1).astype(jnp.int32)
    tile_count = draw_tile_count(jax.random.fold_in(key_list[6], 71), part)
    bias = jnp.clip(-0.5 + 0.3 * jax.random.uniform(key_list[5], (LAYERS * NEURONS,), jnp.float32) ** block_scale(key_list[5], (LAYERS * NEURONS,), ((0, 16),), -0.2, 0.2), -0.5, -0.2)
    return dict(held=held, tile_values=tile_values, tile_rows=tile_rows, tile_cols=tile_cols, tile_count=tile_count, bias=bias)


def layer_slab(full_input, rows_list, cols_list, live_count, values_list, bias_slab):
    batch_rows = full_input.shape[0]
    blocks = full_input.reshape(batch_rows, NTILES, TILE)
    picked = jnp.take(blocks, rows_list, axis=1)
    products = jnp.einsum("bck,ckj->cbj", picked.astype(jnp.float32), values_list.astype(jnp.float32))
    live = jnp.arange(CAP, dtype=jnp.int32) < live_count
    masked = jnp.where(live[:, None, None], products, jnp.zeros_like(products))
    summed = jax.ops.segment_sum(masked, cols_list, num_segments=COLT)
    summed = summed.transpose(1, 0, 2).reshape(batch_rows, COLT * TILE)
    return jnp.maximum(summed + bias_slab[None, :], 0.0).astype(jnp.bfloat16)


def reference(held, tile_values, tile_rows, tile_cols, tile_count, bias):
    devices_all = LAYERS * SPLIT
    values_all = tile_values.reshape(devices_all, CAP, TILE, TILE)
    rows_all = tile_rows.reshape(devices_all, CAP)
    cols_all = tile_cols.reshape(devices_all, CAP)
    bias_all = bias.reshape(devices_all, SLAB)
    indices = jnp.arange(devices_all, dtype=jnp.int32)
    current = held
    outputs = held
    for tick_index in range(TICKS):
        inputs_all = current.reshape(LAYERS, SPLIT, BATCH, SLAB).transpose(0, 2, 1, 3).reshape(LAYERS, BATCH, NEURONS)

        def device_layer(packed):
            index, values_list, rows_list, cols_list, live_count, bias_slab = packed
            full_input = inputs_all[index // SPLIT]
            return layer_slab(full_input, rows_list, cols_list, live_count, values_list, bias_slab)

        outputs = lax.map(device_layer, (indices, values_all, rows_all, cols_all, tile_count, bias_all))
        if tick_index + 1 < TICKS:
            current = jnp.roll(outputs, SPLIT, axis=0)
    return outputs
```

```python
import functools

import jax
import jax.numpy as jnp
from jax import lax
from jax.experimental import pallas as pl
from jax.experimental.pallas import tpu as pltpu
from jax.sharding import PartitionSpec as P

TILE = 128
SPLIT = 8
TICKS = 2
UNROLL = 8


def flipped(array, bit):
    peers = lax.axis_size("section")
    return lax.ppermute(array, "section", [(i, i ^ bit) for i in range(peers)])


def from_behind(array):
    peers = lax.axis_size("section")
    return lax.ppermute(array, "section", [(i, (i + SPLIT) % peers) for i in range(peers)])


def slot_lists(rows, cols, count, position, slab_tiles, trash):
    slots = rows.shape[0]
    index = jnp.arange(slots, dtype=jnp.int32)
    live = index < count
    group = jnp.where(live, (rows // slab_tiles) ^ position, SPLIT)
    member = group[:, None] == jnp.arange(SPLIT, dtype=jnp.int32)[None, :]
    steps = (jnp.sum(member, axis=0, dtype=jnp.int32) + UNROLL - 1) // UNROLL
    lower = jnp.arange(SPLIT + 1)[:, None] > jnp.arange(SPLIT)[None, :]
    starts = jnp.sum(jnp.where(lower, steps[None, :], 0), axis=1, dtype=jnp.int32)
    before = (group[None, :] == group[:, None]) & (index[None, :] < index[:, None])
    rank = jnp.sum(before, axis=1, dtype=jnp.int32)
    base = jnp.sum(jnp.where(member, starts[None, :SPLIT] * UNROLL, 0), axis=1, dtype=jnp.int32)
    place = jnp.where(live, base + rank, -1)
    length = slots + SPLIT * UNROLL
    hit = place[None, :] == jnp.arange(length, dtype=jnp.int32)[:, None]
    empty = trash
    word = (index * 64 + rows % slab_tiles) * 64 + cols
    packed = jnp.sum(jnp.where(hit, (word - empty)[None, :], 0), axis=1, dtype=jnp.int32) + empty
    return starts, packed


def slab_kernel(groups, first, last, starts_ref, list_ref, w_ref, *refs):
    refs = list(refs)
    acc_in = None if first else refs.pop(0)
    bias_ref = refs.pop(0) if last else None
    pieces = [[refs.pop(0) for _ in range(n)] for _, n in groups]
    out_ref = refs.pop(0)
    acc = refs.pop(0) if last else out_ref
    if first:
        acc[...] = jnp.zeros_like(acc)
    else:
        acc[...] = acc_in[...]
    for (group, _), parts in zip(groups, pieces):

        def step(it, carry, parts=parts):
            products = []
            places = []
            for u in range(UNROLL):
                word = list_ref[it * UNROLL + u]
                at = pl.ds(pl.multiple_of(((word >> 6) & 63) * TILE, TILE), TILE)
                rows = [part[:, at] for part in parts]
                x = rows[0] if len(rows) == 1 else jnp.concatenate(rows, axis=0)
                products.append(jnp.dot(x, w_ref[word >> 12], preferred_element_type=jnp.float32))
                places.append(word & 63)
            for place, product in zip(places, products):
                acc[place] = acc[place] + product
            return carry

        lax.fori_loop(starts_ref[group], starts_ref[group + 1], step, 0)
    if last:
        for c in range(out_ref.shape[1] // TILE):
            at = slice(c * TILE, (c + 1) * TILE)
            out_ref[:, at] = jnp.maximum(acc[c] + bias_ref[:, at], 0.0).astype(out_ref.dtype)


def slab_step(groups, starts, packed, weights, acc, bias, pieces):
    first, last = acc is None, bias is not None
    tall = sum(piece.shape[0] for piece in pieces[0])
    wide = pieces[0][0].shape[1]
    smem = pl.BlockSpec(memory_space=pltpu.SMEM)
    vmem = pl.BlockSpec(memory_space=pltpu.VMEM)
    operands = [starts, packed, weights]
    if not first:
        operands.append(acc)
    if last:
        operands.append(bias)
    for parts in pieces:
        operands.extend(parts)
    shape = (wide // TILE + 1, tall, TILE)
    if last:
        out = jax.ShapeDtypeStruct((tall, wide), jnp.bfloat16)
        scratch = [pltpu.VMEM(shape, jnp.float32)]
    else:
        out = jax.ShapeDtypeStruct(shape, jnp.float32)
        scratch = []
    layout = tuple((g, len(parts)) for g, parts in zip(groups, pieces))
    share = len(groups) / SPLIT
    return pl.pallas_call(
        functools.partial(slab_kernel, layout, first, last),
        out_shape=out,
        in_specs=[smem, smem] + [vmem] * (len(operands) - 2),
        out_specs=vmem,
        scratch_shapes=scratch,
        compiler_params=pltpu.CompilerParams(vmem_limit_bytes=4 << 20),
        cost_estimate=pl.CostEstimate(
            flops=int(share * 2 * weights.size * tall * 8),
            bytes_accessed=int(share * weights.size * 2),
            transcendentals=0,
        ),
        name="slab_" + "".join(str(g) for g in groups),
    )(*operands)


def on_device(held, tile_values, tile_rows, tile_cols, tile_count, bias):
    position = lax.axis_index("section") % SPLIT
    wide = held.shape[2]
    starts, packed = slot_lists(tile_rows, tile_cols, tile_count[0], position, wide // TILE, wide // TILE)
    bias_row = bias[None, :]
    own = held[0]
    half = own.shape[0] // 2

    def finish(pieces):
        early = [0, 1, 2, 3, 4, 5]
        late = [6, 7]
        acc = slab_step(early, starts, packed, tile_values, None, None, [pieces[g] for g in early])
        return slab_step(late, starts, packed, tile_values, acc, bias_row, [pieces[g] for g in late])

    outs = []
    for own_half in (own[:half], own[half:]):
        quarter = own_half.shape[0] // 2
        core = flipped(own_half, 1)
        x = flipped(own_half, 2)
        z = flipped(own_half, 4)
        d0 = flipped(x[:quarter], 4)
        d1 = flipped(z[quarter:], 2)
        xc = flipped(x, 1)
        zc = flipped(z, 1)
        d0c = flipped(d0, 1)
        d1c = flipped(d1, 1)
        outs.append(finish([[own_half], [core], [x], [xc], [z], [zc], [d0, d1], [d0c, d1c]]))
    results = []
    for out in outs:
        mine = from_behind(out)
        core = flipped(mine, 1)
        z = flipped(mine, 4)
        x = flipped(mine, 2)
        d = flipped(z, 2)
        zc = flipped(z, 1)
        xc = flipped(x, 1)
        dc = flipped(d, 1)
        results.append(finish([[mine], [core], [x], [xc], [z], [zc], [d], [dc]]))
    return jnp.concatenate(results, axis=0)[None]


def solution(mesh):
    return jax.shard_map(
        on_device,
        mesh=mesh,
        in_specs=(
            P("section", "groups", None),
            P("section", None, None),
            P("section"),
            P("section"),
            P("section"),
            P("section"),
        ),
        out_specs=P("section", "groups", None),
        check_vma=False,
    )
```

```python
import functools

import jax
import jax.numpy as jnp
from jax import lax
from jax.experimental import pallas as pl
from jax.experimental.pallas import tpu as pltpu
from jax.sharding import PartitionSpec as P

TILE = 128
SPLIT = 8
TICKS = 2
UNROLL = 16
CHUNKS = 2

CORE, X, Z = 1, 2, 4


def sent(array, target):
    peers = lax.axis_size("section")
    return lax.ppermute(array, "section", [(i, target(i, peers)) for i in range(peers)])


def across_core(array):
    return sent(array, lambda i, n: i ^ CORE)


def across_first(array):
    return sent(array, lambda i, n: i ^ (Z if i & CORE else X))


def across_second(array):
    return sent(array, lambda i, n: i ^ (X if i & CORE else Z))


def from_behind(array):
    return sent(array, lambda i, n: (i + SPLIT) % n)


def after(array, *others):
    return lax.optimization_barrier((array, *others))[0]


PLACE = ((0, 1, 2, 5, 3, 4, 6, 7), (0, 1, 3, 4, 2, 5, 6, 7))


def slab_place(source, position):
    difference = source ^ position
    odd = (position & CORE) == 1
    even_place = sum(jnp.where(difference == j, PLACE[0][j], 0) for j in range(SPLIT))
    odd_place = sum(jnp.where(difference == j, PLACE[1][j], 0) for j in range(SPLIT))
    return jnp.where(odd, odd_place, even_place)


def slot_lists(phases, place, chunk, tile, cols, live, spare):
    slots = cols.shape[0]
    index = jnp.arange(slots, dtype=jnp.int32)
    count = len(phases)
    phase = jnp.full((slots,), count, jnp.int32)
    block = jnp.zeros((slots,), jnp.int32)
    for k, blocks in enumerate(phases):
        for at, (p, c) in enumerate(blocks):
            hit = live & (place == p) & (chunk == c)
            phase = jnp.where(hit, k, phase)
            block = jnp.where(hit, at, block)
    member = phase[:, None] == jnp.arange(count, dtype=jnp.int32)[None, :]
    steps = (jnp.sum(member, axis=0, dtype=jnp.int32) + UNROLL - 1) // UNROLL
    lower = jnp.arange(count + 1)[:, None] > jnp.arange(count)[None, :]
    starts = jnp.sum(jnp.where(lower, steps[None, :], 0), axis=1, dtype=jnp.int32)
    before = (phase[None, :] == phase[:, None]) & (index[None, :] < index[:, None])
    rank = jnp.sum(before, axis=1, dtype=jnp.int32)
    base = jnp.sum(jnp.where(member, starts[None, :count] * UNROLL, 0), axis=1, dtype=jnp.int32)
    spot = jnp.where(live, base + rank, -1)
    hit = spot[None, :] == jnp.arange(slots + count * UNROLL, dtype=jnp.int32)[:, None]
    word = ((index * 32 + block) * 64 + tile) * 64 + cols
    packed = jnp.sum(jnp.where(hit, (word - spare)[None, :], 0), axis=1, dtype=jnp.int32) + spare
    return starts, packed


def phase_kernel(phase, pieces, first, last, starts_ref, list_ref, w_ref, *refs):
    refs = list(refs)
    acc_in = None if first else refs.pop(0)
    bias_ref = refs.pop(0) if last else None
    piece_refs = [refs.pop(0) for _ in range(pieces)]
    outs = [refs.pop(0) for _ in range(last)] if last else []
    acc = None if last else refs.pop(0)
    held = refs.pop(0)
    if last:
        acc = refs.pop(0)
    for at, piece in enumerate(piece_refs):
        held[at] = piece[...]
    acc[...] = jnp.zeros_like(acc) if first else acc_in[...]

    def step(it, carry):
        products = []
        places = []
        for u in range(UNROLL):
            word = list_ref[it * UNROLL + u]
            at = pl.ds(pl.multiple_of(((word >> 6) & 63) * TILE, TILE), TILE)
            x = held[(word >> 12) & 31, :, at]
            products.append(jnp.dot(x, w_ref[word >> 17], preferred_element_type=jnp.float32))
            places.append(word & 63)
        for place, product in zip(places, products):
            acc[place] = acc[place] + product
        return carry

    lax.fori_loop(starts_ref[phase], starts_ref[phase + 1], step, 0)
    c = 0
    for out in outs:
        for k in range(out.shape[1] // TILE):
            at = slice(c * TILE, (c + 1) * TILE)
            out[:, k * TILE:(k + 1) * TILE] = jnp.maximum(acc[c] + bias_ref[:, at], 0.0).astype(out.dtype)
            c += 1


def run_phase(phase, lists, weights, acc, pieces, wide, bias=None, chunks=0):
    first, last = acc is None, bias is not None
    tall, piece_wide = pieces[0].shape
    smem = pl.BlockSpec(memory_space=pltpu.SMEM)
    vmem = pl.BlockSpec(memory_space=pltpu.VMEM)
    operands = [*lists, weights] + ([] if first else [acc]) + ([bias] if last else []) + list(pieces)
    shape = (wide // TILE + 1, tall, TILE)
    scratch = [pltpu.VMEM((len(pieces), tall, piece_wide), jnp.bfloat16)]
    aliases = {}
    if last:
        out = [jax.ShapeDtypeStruct((tall, wide // chunks), jnp.bfloat16)] * chunks
        scratch.append(pltpu.VMEM(shape, jnp.float32))
    else:
        out = [jax.ShapeDtypeStruct(shape, jnp.float32)]
        if not first:
            aliases = {3: 0}
    results = pl.pallas_call(
        functools.partial(phase_kernel, phase, len(pieces), first, chunks if last else 0),
        out_shape=out,
        in_specs=[smem, smem] + [vmem] * (len(operands) - 2),
        out_specs=[vmem] * len(out),
        scratch_shapes=scratch,
        input_output_aliases=aliases,
        compiler_params=pltpu.CompilerParams(vmem_limit_bytes=12 << 20),
        cost_estimate=pl.CostEstimate(flops=2_000_000_000, bytes_accessed=6_000_000, transcendentals=0),
        name=f"phase_{phase}",
    )(*operands)
    return results if last else results[0]


FIRST_PHASES = (
    ((0, 0), (1, 0)),
    ((2, 0), (3, 0), (4, 0), (5, 0)),
    ((6, 0), (7, 0)),
)
LATER_PHASES = (
    tuple((p, 0) for p in range(8)),
    tuple((p, 1) for p in range(6)),
    ((6, 1), (7, 1)),
)


def first_layer(own, lists, weights, bias):
    wide = own.shape[1]
    a = across_first(own)
    core = across_core(own)
    b = across_second(own)
    acc = run_phase(0, lists, weights, None, [own, core], wide)
    a = after(a, acc)
    e = across_second(a)
    pieces = [a, b, across_core(a), across_core(b)]
    acc = run_phase(1, lists, weights, acc, pieces, wide)
    e = after(e, acc)
    return run_phase(2, lists, weights, acc, [e, across_core(e)], wide, bias, CHUNKS)


def later_layer(parts, lists, weights, bias, wide, chunks):
    parts = [from_behind(part) for part in parts]
    acc = None
    for at, own in enumerate(parts):
        a = across_first(own)
        b = across_second(own)
        core = across_core(own)
        e = across_second(a)
        pieces = [own, core, a, b, across_core(a), across_core(b)]
        if at == 0:
            acc = run_phase(0, lists, weights, None, [*pieces, e, across_core(e)], wide)
        else:
            e = after(e, acc)
            acc = run_phase(1, lists, weights, acc, pieces, wide)
            return run_phase(2, lists, weights, acc, [e, across_core(e)], wide, bias, chunks)


def on_device(held, tile_values, tile_rows, tile_cols, tile_count, bias):
    position = lax.axis_index("section") % SPLIT
    own = held[0]
    wide = own.shape[1]
    tiles = wide // TILE
    live = jnp.arange(tile_rows.shape[0], dtype=jnp.int32) < tile_count[0]
    place = slab_place(tile_rows // tiles, position)
    tile = tile_rows % tiles
    part = tiles // CHUNKS
    first_lists = slot_lists(FIRST_PHASES, place, jnp.zeros_like(tile), tile, tile_cols, live, tiles)
    later_lists = slot_lists(LATER_PHASES, place, tile // part, tile % part, tile_cols, live, tiles)
    bias_row = bias[None, :]
    slab = first_layer(own, first_lists, tile_values, bias_row)
    for tick in range(1, TICKS):
        last = tick + 1 == TICKS
        slab = later_layer(slab, later_lists, tile_values, bias_row, wide, 1 if last else CHUNKS)
    return slab[0][None]


def solution(mesh):
    return jax.shard_map(
        on_device,
        mesh=mesh,
        in_specs=(
            P("section", "groups", None),
            P("section", None, None),
            P("section"),
            P("section"),
            P("section"),
            P("section"),
        ),
        out_specs=P("section", "groups", None),
        check_vma=False,
    )
```

```python
import functools

import jax
import jax.numpy as jnp
from jax import lax
from jax.experimental import pallas as pl
from jax.experimental.pallas import tpu as pltpu
from jax.sharding import PartitionSpec as P

TILE = 128
SPLIT = 8
TICKS = 2
UNROLL = 16
CHUNKS = 2

CORE, X, Z = 1, 2, 4


def sent(array, name, target):
    peers = lax.axis_size("section")
    with jax.named_scope(name):
        return lax.ppermute(array, "section", [(i, target(i, peers)) for i in range(peers)])


def across_core(array, name):
    return sent(array, name, lambda i, n: i ^ CORE)


def across_first(array, name):
    return sent(array, name, lambda i, n: i ^ (Z if i & CORE else X))


def across_second(array, name):
    return sent(array, name, lambda i, n: i ^ (X if i & CORE else Z))


def from_behind(array, name):
    return sent(array, name, lambda i, n: (i + SPLIT) % n)


def after(array, *others):
    return lax.optimization_barrier((array, *others))[0]


PLACE = ((0, 1, 2, 5, 3, 4, 6, 7), (0, 1, 3, 4, 2, 5, 6, 7))


def slab_place(source, position):
    difference = source ^ position
    odd = (position & CORE) == 1
    even_place = sum(jnp.where(difference == j, PLACE[0][j], 0) for j in range(SPLIT))
    odd_place = sum(jnp.where(difference == j, PLACE[1][j], 0) for j in range(SPLIT))
    return jnp.where(odd, odd_place, even_place)


def slot_lists(phases, place, chunk, tile, cols, live, spare):
    slots = cols.shape[0]
    index = jnp.arange(slots, dtype=jnp.int32)
    count = len(phases)
    phase = jnp.full((slots,), count, jnp.int32)
    block = jnp.zeros((slots,), jnp.int32)
    for k, blocks in enumerate(phases):
        for p, c, at in blocks:
            hit = live & (place == p) & (chunk == c)
            phase = jnp.where(hit, k, phase)
            block = jnp.where(hit, at, block)
    member = phase[:, None] == jnp.arange(count, dtype=jnp.int32)[None, :]
    steps = (jnp.sum(member, axis=0, dtype=jnp.int32) + UNROLL - 1) // UNROLL
    lower = jnp.arange(count + 1)[:, None] > jnp.arange(count)[None, :]
    starts = jnp.sum(jnp.where(lower, steps[None, :], 0), axis=1, dtype=jnp.int32)
    before = (phase[None, :] == phase[:, None]) & (index[None, :] < index[:, None])
    rank = jnp.sum(before, axis=1, dtype=jnp.int32)
    base = jnp.sum(jnp.where(member, starts[None, :count] * UNROLL, 0), axis=1, dtype=jnp.int32)
    spot = jnp.where(live, base + rank, -1)
    hit = spot[None, :] == jnp.arange(slots + count * UNROLL, dtype=jnp.int32)[:, None]
    word = ((index * 32 + block) * 64 + tile) * 64 + cols
    packed = jnp.sum(jnp.where(hit, (word - spare)[None, :], 0), axis=1, dtype=jnp.int32) + spare
    return starts, packed


def phase_kernel(phase, pieces, first, columns, starts_ref, list_ref, w_ref, *refs):
    refs = list(refs)
    if not first:
        refs.pop(0)
    bias_ref = refs.pop(0) if columns else None
    piece_refs = [refs.pop(0) for _ in range(pieces)]
    acc = refs.pop(0)
    out = refs.pop(0) if columns else None
    held = refs.pop(0)
    rows = held.shape[1]
    at = 0
    for piece in piece_refs:
        for row in range(0, piece.shape[0], rows):
            held[at] = piece[row:row + rows]
            at += 1
    if first:
        acc[...] = jnp.zeros_like(acc)

    def step(it, carry):
        products = []
        places = []
        for u in range(UNROLL):
            word = list_ref[it * UNROLL + u]
            at = pl.ds(pl.multiple_of(((word >> 6) & 63) * TILE, TILE), TILE)
            x = held[(word >> 12) & 31, :, at]
            products.append(jnp.dot(x, w_ref[word >> 17], preferred_element_type=jnp.float32))
            places.append(word & 63)
        for place, product in zip(places, products):
            acc[place] = acc[place] + product
        return carry

    lax.fori_loop(starts_ref[phase], starts_ref[phase + 1], step, 0)
    for k, c in enumerate(columns):
        at = slice(c * TILE, (c + 1) * TILE)
        out[:, k * TILE:(k + 1) * TILE] = jnp.maximum(acc[c] + bias_ref[:, at], 0.0).astype(out.dtype)


def run_phase(phase, lists, weights, acc, pieces, wide, bias=None, columns=()):
    first, last = acc is None, bias is not None
    tall, piece_wide = pieces[0].shape
    slabs = sum(piece.shape[0] for piece in pieces) // tall
    smem = pl.BlockSpec(memory_space=pltpu.SMEM)
    vmem = pl.BlockSpec(memory_space=pltpu.VMEM)
    operands = [*lists, weights] + ([] if first else [acc]) + ([bias] if last else []) + list(pieces)
    shape = (wide // TILE + 1, tall, TILE)
    scratch = [pltpu.VMEM((slabs, tall, piece_wide), jnp.bfloat16)]
    out = [jax.ShapeDtypeStruct(shape, jnp.float32)]
    if last:
        out.append(jax.ShapeDtypeStruct((tall, len(columns) * TILE), jnp.bfloat16))
    aliases = {} if first else {3: 0}
    results = pl.pallas_call(
        functools.partial(phase_kernel, phase, len(pieces), first, tuple(columns)),
        out_shape=out,
        in_specs=[smem, smem] + [vmem] * (len(operands) - 2),
        out_specs=[vmem] * len(out),
        scratch_shapes=scratch,
        input_output_aliases=aliases,
        compiler_params=pltpu.CompilerParams(vmem_limit_bytes=12 << 20),
        cost_estimate=pl.CostEstimate(flops=2_000_000_000, bytes_accessed=6_000_000, transcendentals=0),
        name=f"phase_{phase}",
    )(*operands)
    return results if last else results[0]


def blocks(*slabs, columns=None):
    if columns is None:
        return tuple((place, chunk, at) for at, (place, chunk) in enumerate(slabs))
    return tuple((place, chunk, at) for at, place in enumerate(slabs) for chunk in columns)


ALL = tuple(range(CHUNKS))
FIRST_PHASES = (
    blocks(0, 1, columns=ALL),
    blocks(2, 3, 4, 5, columns=ALL),
) + tuple(blocks(6, 7, columns=(k,)) for k in ALL)
LATER_PHASES = (
    blocks(*((p, 0) for p in range(6))),
    blocks((6, 0), (7, 0), *((p, 1) for p in range(6))),
    blocks((6, 1), (7, 1)),
)


def first_layer(own, lists, weights, bias):
    wide = own.shape[1]
    a = across_first(own, "a")
    core = across_core(own, "core")
    b = across_second(own, "b")
    acc = run_phase(0, lists, weights, None, [own, core], wide)
    a = after(a, acc)
    e = across_second(a, "e")
    pieces = [a, b, across_core(a, "ac"), across_core(b, "bc")]
    acc = run_phase(1, lists, weights, acc, pieces, wide)
    e = after(e, acc)
    pieces = [e, across_core(e, "ec")]
    outs = []
    part = wide // TILE // CHUNKS
    for k in ALL:
        acc, out = run_phase(2 + k, lists, weights, acc, pieces, wide, bias, range(k * part, (k + 1) * part))
        outs.append(out)
    return outs


def later_layer(parts, lists, weights, bias, wide):
    done = parts[-1]
    parts = [from_behind(part, f"cross{k}") for k, part in enumerate(parts)]
    parts[0] = after(parts[0], done)
    acc, late = None, []
    for k, own in enumerate(parts):
        a = across_first(own, f"A{k}")
        b = across_second(own, f"B{k}")
        core = across_core(own, f"CORE{k}")
        e = across_second(a, f"E{k}")
        pieces = [*late, own, core, a, b, across_core(a, f"AC{k}"), across_core(b, f"BC{k}")]
        if k:
            e = after(e, acc)
        late = [e, across_core(e, f"EC{k}")]
        acc = run_phase(k, lists, weights, acc, pieces, wide)
    return run_phase(len(parts), lists, weights, acc, late, wide, bias, range(wide // TILE))[1]


def on_device(held, tile_values, tile_rows, tile_cols, tile_count, bias):
    position = lax.axis_index("section") % SPLIT
    own = held[0]
    wide = own.shape[1]
    tiles = wide // TILE
    live = jnp.arange(tile_rows.shape[0], dtype=jnp.int32) < tile_count[0]
    place = slab_place(tile_rows // tiles, position)
    tile = tile_rows % tiles
    part = tiles // CHUNKS
    first_lists = slot_lists(FIRST_PHASES, place, tile_cols // part, tile, tile_cols, live, tiles)
    later_lists = slot_lists(LATER_PHASES, place, tile // part, tile % part, tile_cols, live, tiles)
    bias_row = bias[None, :]
    parts = first_layer(own, first_lists, tile_values, bias_row)
    for tick in range(1, TICKS):
        slab = later_layer(parts, later_lists, tile_values, bias_row, wide)
        parts = jnp.split(slab, CHUNKS, axis=1)
    return slab[None]


def solution(mesh):
    return jax.shard_map(
        on_device,
        mesh=mesh,
        in_specs=(
            P("section", "groups", None),
            P("section", None, None),
            P("section"),
            P("section"),
            P("section"),
            P("section"),
        ),
        out_specs=P("section", "groups", None),
        check_vma=False,
    )
```

```python
import functools

import jax
import jax.numpy as jnp
from jax import lax
from jax.experimental import pallas as pl
from jax.experimental.pallas import tpu as pltpu
from jax.sharding import PartitionSpec as P

TILE = 128
SPLIT = 8
TICKS = 2
UNROLL = 16
CHUNKS = 2

CORE, X, Z = 1, 2, 4


def sent(array, name, target):
    peers = lax.axis_size("section")
    with jax.named_scope(name):
        return lax.ppermute(array, "section", [(i, target(i, peers)) for i in range(peers)])


def across_core(array, name):
    return sent(array, name, lambda i, n: i ^ CORE)


def across_first(array, name):
    return sent(array, name, lambda i, n: i ^ (Z if i & CORE else X))


def across_second(array, name):
    return sent(array, name, lambda i, n: i ^ (X if i & CORE else Z))


def from_behind(array, name):
    return sent(array, name, lambda i, n: (i + SPLIT) % n)


def after(array, *others):
    return lax.optimization_barrier((array, *others))[0]


PLACE = ((0, 1, 2, 5, 3, 4, 6, 7), (0, 1, 3, 4, 2, 5, 6, 7))


def slab_place(source, position):
    difference = source ^ position
    odd = (position & CORE) == 1
    even_place = sum(jnp.where(difference == j, PLACE[0][j], 0) for j in range(SPLIT))
    odd_place = sum(jnp.where(difference == j, PLACE[1][j], 0) for j in range(SPLIT))
    return jnp.where(odd, odd_place, even_place)


def slot_lists(phases, place, chunk, tile, cols, live, spare):
    slots = cols.shape[0]
    index = jnp.arange(slots, dtype=jnp.int32)
    count = len(phases)
    phase = jnp.full((slots,), count, jnp.int32)
    block = jnp.zeros((slots,), jnp.int32)
    for k, blocks in enumerate(phases):
        for p, c, at in blocks:
            hit = live & (place == p) & (chunk == c)
            phase = jnp.where(hit, k, phase)
            block = jnp.where(hit, at, block)
    member = phase[:, None] == jnp.arange(count, dtype=jnp.int32)[None, :]
    steps = (jnp.sum(member, axis=0, dtype=jnp.int32) + UNROLL - 1) // UNROLL
    lower = jnp.arange(count + 1)[:, None] > jnp.arange(count)[None, :]
    starts = jnp.sum(jnp.where(lower, steps[None, :], 0), axis=1, dtype=jnp.int32)
    before = (phase[None, :] == phase[:, None]) & (index[None, :] < index[:, None])
    rank = jnp.sum(before, axis=1, dtype=jnp.int32)
    base = jnp.sum(jnp.where(member, starts[None, :count] * UNROLL, 0), axis=1, dtype=jnp.int32)
    spot = jnp.where(live, base + rank, -1)
    hit = spot[None, :] == jnp.arange(slots + count * UNROLL, dtype=jnp.int32)[:, None]
    word = ((index * 32 + block) * 64 + tile) * 64 + cols
    packed = jnp.sum(jnp.where(hit, (word - spare)[None, :], 0), axis=1, dtype=jnp.int32) + spare
    return starts, packed


def phase_kernel(phase, pieces, first, columns, starts_ref, list_ref, w_ref, *refs):
    refs = list(refs)
    if not first:
        refs.pop(0)
    bias_ref = refs.pop(0) if columns else None
    piece_refs = [refs.pop(0) for _ in range(pieces)]
    acc = refs.pop(0)
    out = refs.pop(0) if columns else None
    held = refs.pop(0)
    rows = held.shape[1]
    at = 0
    for piece in piece_refs:
        for row in range(0, piece.shape[0], rows):
            held[at] = piece[row:row + rows]
            at += 1
    if first:
        acc[...] = jnp.zeros_like(acc)

    def step(it, carry):
        products = []
        places = []
        for u in range(UNROLL):
            word = list_ref[it * UNROLL + u]
            at = pl.ds(pl.multiple_of(((word >> 6) & 63) * TILE, TILE), TILE)
            x = held[(word >> 12) & 31, :, at]
            products.append(jnp.dot(x, w_ref[word >> 17], preferred_element_type=jnp.float32))
            places.append(word & 63)
        for place, product in zip(places, products):
            acc[place] = acc[place] + product
        return carry

    lax.fori_loop(starts_ref[phase], starts_ref[phase + 1], step, 0)
    for k, c in enumerate(columns):
        at = slice(c * TILE, (c + 1) * TILE)
        out[:, k * TILE:(k + 1) * TILE] = jnp.maximum(acc[c] + bias_ref[:, at], 0.0).astype(out.dtype)


def run_phase(phase, lists, weights, acc, pieces, wide, bias=None, columns=()):
    first, last = acc is None, bias is not None
    tall, piece_wide = pieces[0].shape
    slabs = sum(piece.shape[0] for piece in pieces) // tall
    smem = pl.BlockSpec(memory_space=pltpu.SMEM)
    vmem = pl.BlockSpec(memory_space=pltpu.VMEM)
    operands = [*lists, weights] + ([] if first else [acc]) + ([bias] if last else []) + list(pieces)
    shape = (wide // TILE + 1, tall, TILE)
    scratch = [pltpu.VMEM((slabs, tall, piece_wide), jnp.bfloat16)]
    out = [jax.ShapeDtypeStruct(shape, jnp.float32)]
    if last:
        out.append(jax.ShapeDtypeStruct((tall, len(columns) * TILE), jnp.bfloat16))
    aliases = {} if first else {3: 0}
    results = pl.pallas_call(
        functools.partial(phase_kernel, phase, len(pieces), first, tuple(columns)),
        out_shape=out,
        in_specs=[smem, smem] + [vmem] * (len(operands) - 2),
        out_specs=[vmem] * len(out),
        scratch_shapes=scratch,
        input_output_aliases=aliases,
        compiler_params=pltpu.CompilerParams(vmem_limit_bytes=12 << 20),
        cost_estimate=pl.CostEstimate(flops=2_000_000_000, bytes_accessed=6_000_000, transcendentals=0),
        name=f"phase_{phase}",
    )(*operands)
    return results if last else results[0]


def blocks(*slabs, columns=None):
    if columns is None:
        return tuple((place, chunk, at) for at, (place, chunk) in enumerate(slabs))
    return tuple((place, chunk, at) for at, place in enumerate(slabs) for chunk in columns)


ALL = tuple(range(CHUNKS))
FIRST_PHASES = (
    blocks(0, 1, columns=ALL),
    blocks(2, 3, 4, 5, columns=ALL),
) + tuple(blocks(6, 7, columns=(k,)) for k in ALL)
LATER_PHASES = (
    blocks((0, 0), (1, 0)),
    blocks(*((p, 0) for p in range(2, 6))),
    blocks((6, 0), (7, 0), *((p, 1) for p in range(6))),
    blocks((6, 1), (7, 1)),
)


def first_layer(own, lists, weights, bias):
    wide = own.shape[1]
    a = across_first(own, "a")
    core = across_core(own, "core")
    b = across_second(own, "b")
    acc = run_phase(0, lists, weights, None, [own, core], wide)
    a = after(a, acc)
    e = across_second(a, "e")
    pieces = [a, b, across_core(a, "ac"), across_core(b, "bc")]
    acc = run_phase(1, lists, weights, acc, pieces, wide)
    e = after(e, acc)
    pieces = [e, across_core(e, "ec")]
    outs = []
    part = wide // TILE // CHUNKS
    for k in ALL:
        acc, out = run_phase(2 + k, lists, weights, acc, pieces, wide, bias, range(k * part, (k + 1) * part))
        outs.append(out)
    return outs


def later_layer(parts, lists, weights, bias, wide):
    done = parts[-1]
    parts = [from_behind(part, f"cross{k}") for k, part in enumerate(parts)]
    parts[0] = after(parts[0], done)
    core = [across_core(part, f"CORE{k}") for k, part in enumerate(parts[:1])]
    acc = run_phase(0, lists, weights, None, [parts[0], core[0]], wide)
    core.append(across_core(parts[1], "CORE1"))
    late = []
    for k, own in enumerate(parts):
        a = across_first(own, f"A{k}")
        b = across_second(own, f"B{k}")
        if k == 0:
            a = after(a, acc)
        e = across_second(a, f"E{k}")
        pieces = [*late, *([own, core[k]] if k else []), a, b, across_core(a, f"AC{k}"), across_core(b, f"BC{k}")]
        if k:
            e = after(e, acc)
        late = [e, across_core(e, f"EC{k}")]
        acc = run_phase(k + 1, lists, weights, acc, pieces, wide)
    return run_phase(3, lists, weights, acc, late, wide, bias, range(wide // TILE))[1]


def on_device(held, tile_values, tile_rows, tile_cols, tile_count, bias):
    position = lax.axis_index("section") % SPLIT
    own = held[0]
    wide = own.shape[1]
    tiles = wide // TILE
    live = jnp.arange(tile_rows.shape[0], dtype=jnp.int32) < tile_count[0]
    place = slab_place(tile_rows // tiles, position)
    tile = tile_rows % tiles
    part = tiles // CHUNKS
    first_lists = slot_lists(FIRST_PHASES, place, tile_cols // part, tile, tile_cols, live, tiles)
    later_lists = slot_lists(LATER_PHASES, place, tile // part, tile % part, tile_cols, live, tiles)
    bias_row = bias[None, :]
    parts = first_layer(own, first_lists, tile_values, bias_row)
    for tick in range(1, TICKS):
        slab = later_layer(parts, later_lists, tile_values, bias_row, wide)
        parts = jnp.split(slab, CHUNKS, axis=1)
    return slab[None]


def solution(mesh):
    return jax.shard_map(
        on_device,
        mesh=mesh,
        in_specs=(
            P("section", "groups", None),
            P("section", None, None),
            P("section"),
            P("section"),
            P("section"),
            P("section"),
        ),
        out_specs=P("section", "groups", None),
        check_vma=False,
    )
```

```python
import functools

import jax
import jax.numpy as jnp
from jax import lax
from jax.experimental import pallas as pl
from jax.experimental.pallas import tpu as pltpu
from jax.sharding import PartitionSpec as P

TILE = 128
SPLIT = 8
TICKS = 2
UNROLL = 32
CHUNKS = 2

CORE, X, Z = 1, 2, 4


def sent(array, name, target):
    peers = lax.axis_size("section")
    with jax.named_scope(name):
        return lax.ppermute(array, "section", [(i, target(i, peers)) for i in range(peers)])


def across_core(array, name):
    return sent(array, name, lambda i, n: i ^ CORE)


def across_first(array, name):
    return sent(array, name, lambda i, n: i ^ (Z if i & CORE else X))


def across_second(array, name):
    return sent(array, name, lambda i, n: i ^ (X if i & CORE else Z))


def from_behind(array, name):
    return sent(array, name, lambda i, n: (i + SPLIT) % n)


def after(array, *others):
    return lax.optimization_barrier((array, *others))[0]


PLACE = ((0, 1, 2, 5, 3, 4, 6, 7), (0, 1, 3, 4, 2, 5, 6, 7))


def slab_place(source, position):
    difference = source ^ position
    odd = (position & CORE) == 1
    even_place = sum(jnp.where(difference == j, PLACE[0][j], 0) for j in range(SPLIT))
    odd_place = sum(jnp.where(difference == j, PLACE[1][j], 0) for j in range(SPLIT))
    return jnp.where(odd, odd_place, even_place)


def slot_lists(phases, place, chunk, tile, cols, live, spare):
    slots = cols.shape[0]
    index = jnp.arange(slots, dtype=jnp.int32)
    count = len(phases)
    phase = jnp.full((slots,), count, jnp.int32)
    block = jnp.zeros((slots,), jnp.int32)
    for k, blocks in enumerate(phases):
        for p, c, at in blocks:
            hit = live & (place == p) & (chunk == c)
            phase = jnp.where(hit, k, phase)
            block = jnp.where(hit, at, block)
    member = phase[:, None] == jnp.arange(count, dtype=jnp.int32)[None, :]
    steps = (jnp.sum(member, axis=0, dtype=jnp.int32) + UNROLL - 1) // UNROLL
    lower = jnp.arange(count + 1)[:, None] > jnp.arange(count)[None, :]
    starts = jnp.sum(jnp.where(lower, steps[None, :], 0), axis=1, dtype=jnp.int32)
    before = (phase[None, :] == phase[:, None]) & (index[None, :] < index[:, None])
    rank = jnp.sum(before, axis=1, dtype=jnp.int32)
    base = jnp.sum(jnp.where(member, starts[None, :count] * UNROLL, 0), axis=1, dtype=jnp.int32)
    spot = jnp.where(live, base + rank, -1)
    hit = spot[None, :] == jnp.arange(slots + count * UNROLL, dtype=jnp.int32)[:, None]
    word = ((index * 32 + block) * 64 + tile) * 64 + cols
    packed = jnp.sum(jnp.where(hit, (word - spare)[None, :], 0), axis=1, dtype=jnp.int32) + spare
    return starts, packed


def phase_kernel(phase, pieces, first, columns, starts_ref, list_ref, w_ref, *refs):
    refs = list(refs)
    if not first:
        refs.pop(0)
    bias_ref = refs.pop(0) if columns else None
    piece_refs = [refs.pop(0) for _ in range(pieces)]
    acc = refs.pop(0)
    out = refs.pop(0) if columns else None
    held = refs.pop(0)
    rows = held.shape[1]
    at = 0
    for piece in piece_refs:
        for row in range(0, piece.shape[0], rows):
            held[at] = piece[row:row + rows]
            at += 1
    if first:
        acc[...] = jnp.zeros_like(acc)

    def step(it, carry):
        products = []
        places = []
        for u in range(UNROLL):
            word = list_ref[it * UNROLL + u]
            at = pl.ds(pl.multiple_of(((word >> 6) & 63) * TILE, TILE), TILE)
            x = held[(word >> 12) & 31, :, at]
            products.append(jnp.dot(x, w_ref[word >> 17], preferred_element_type=jnp.float32))
            places.append(word & 63)
        for place, product in zip(places, products):
            acc[place] = acc[place] + product
        return carry

    lax.fori_loop(starts_ref[phase], starts_ref[phase + 1], step, 0)
    for k, c in enumerate(columns):
        at = slice(c * TILE, (c + 1) * TILE)
        out[:, k * TILE:(k + 1) * TILE] = jnp.maximum(acc[c] + bias_ref[:, at], 0.0).astype(out.dtype)


def run_phase(phase, lists, weights, acc, pieces, wide, bias=None, columns=()):
    first, last = acc is None, bias is not None
    tall, piece_wide = pieces[0].shape
    slabs = sum(piece.shape[0] for piece in pieces) // tall
    smem = pl.BlockSpec(memory_space=pltpu.SMEM)
    vmem = pl.BlockSpec(memory_space=pltpu.VMEM)
    operands = [*lists, weights] + ([] if first else [acc]) + ([bias] if last else []) + list(pieces)
    shape = (wide // TILE + 1, tall, TILE)
    scratch = [pltpu.VMEM((slabs, tall, piece_wide), jnp.bfloat16)]
    out = [jax.ShapeDtypeStruct(shape, jnp.float32)]
    if last:
        out.append(jax.ShapeDtypeStruct((tall, len(columns) * TILE), jnp.bfloat16))
    aliases = {} if first else {3: 0}
    results = pl.pallas_call(
        functools.partial(phase_kernel, phase, len(pieces), first, tuple(columns)),
        out_shape=out,
        in_specs=[smem, smem] + [vmem] * (len(operands) - 2),
        out_specs=[vmem] * len(out),
        scratch_shapes=scratch,
        input_output_aliases=aliases,
        compiler_params=pltpu.CompilerParams(vmem_limit_bytes=12 << 20),
        cost_estimate=pl.CostEstimate(flops=2_000_000_000, bytes_accessed=6_000_000, transcendentals=0),
        name=f"phase_{phase}",
    )(*operands)
    return results if last else results[0]


def blocks(*slabs, columns=None):
    if columns is None:
        return tuple((place, chunk, at) for at, (place, chunk) in enumerate(slabs))
    return tuple((place, chunk, at) for at, place in enumerate(slabs) for chunk in columns)


ALL = tuple(range(CHUNKS))
FIRST_PHASES = (
    blocks(0, 1, columns=ALL),
    blocks(2, 3, 4, 5, columns=ALL),
) + tuple(blocks(6, 7, columns=(k,)) for k in ALL)
LATER_PHASES = (
    blocks((0, 0), (1, 0)),
    blocks(*((p, 0) for p in range(2, 6))),
    blocks((6, 0), (7, 0), *((p, 1) for p in range(6))),
    blocks((6, 1), (7, 1)),
)


def first_layer(own, lists, weights, bias):
    wide = own.shape[1]
    a = across_first(own, "a")
    core = across_core(own, "core")
    b = across_second(own, "b")
    acc = run_phase(0, lists, weights, None, [own, core], wide)
    a = after(a, acc)
    e = across_second(a, "e")
    pieces = [a, b, across_core(a, "ac"), across_core(b, "bc")]
    acc = run_phase(1, lists, weights, acc, pieces, wide)
    e = after(e, acc)
    pieces = [e, across_core(e, "ec")]
    outs = []
    part = wide // TILE // CHUNKS
    for k in ALL:
        acc, out = run_phase(2 + k, lists, weights, acc, pieces, wide, bias, range(k * part, (k + 1) * part))
        outs.append(out)
    return outs


def later_layer(parts, lists, weights, bias, wide):
    done = parts[-1]
    parts = [from_behind(part, f"cross{k}") for k, part in enumerate(parts)]
    parts[0] = after(parts[0], done)
    core = [across_core(part, f"CORE{k}") for k, part in enumerate(parts[:1])]
    acc = run_phase(0, lists, weights, None, [parts[0], core[0]], wide)
    core.append(across_core(parts[1], "CORE1"))
    late = []
    for k, own in enumerate(parts):
        a = across_first(own, f"A{k}")
        b = across_second(own, f"B{k}")
        if k == 0:
            a = after(a, acc)
        e = across_second(a, f"E{k}")
        pieces = [*late, *([own, core[k]] if k else []), a, b, across_core(a, f"AC{k}"), across_core(b, f"BC{k}")]
        if k:
            e = after(e, acc)
        late = [e, across_core(e, f"EC{k}")]
        acc = run_phase(k + 1, lists, weights, acc, pieces, wide)
    return run_phase(3, lists, weights, acc, late, wide, bias, range(wide // TILE))[1]


def on_device(held, tile_values, tile_rows, tile_cols, tile_count, bias):
    position = lax.axis_index("section") % SPLIT
    own = held[0]
    wide = own.shape[1]
    tiles = wide // TILE
    live = jnp.arange(tile_rows.shape[0], dtype=jnp.int32) < tile_count[0]
    place = slab_place(tile_rows // tiles, position)
    tile = tile_rows % tiles
    part = tiles // CHUNKS
    first_lists = slot_lists(FIRST_PHASES, place, tile_cols // part, tile, tile_cols, live, tiles)
    later_lists = slot_lists(LATER_PHASES, place, tile // part, tile % part, tile_cols, live, tiles)
    bias_row = bias[None, :]
    parts = first_layer(own, first_lists, tile_values, bias_row)
    for tick in range(1, TICKS):
        slab = later_layer(parts, later_lists, tile_values, bias_row, wide)
        parts = jnp.split(slab, CHUNKS, axis=1)
    return slab[None]


def solution(mesh):
    return jax.shard_map(
        on_device,
        mesh=mesh,
        in_specs=(
            P("section", "groups", None),
            P("section", None, None),
            P("section"),
            P("section"),
            P("section"),
            P("section"),
        ),
        out_specs=P("section", "groups", None),
        check_vma=False,
    )
```

```python
import functools

import jax
import jax.numpy as jnp
from jax import lax
from jax.experimental import pallas as pl
from jax.experimental.pallas import tpu as pltpu
from jax.sharding import PartitionSpec as P

TILE = 128
SPLIT = 8
TICKS = 2
UNROLL = 32
CHUNKS = 2

CORE, X, Z = 1, 2, 4


def sent(array, name, target):
    peers = lax.axis_size("section")
    with jax.named_scope(name):
        return lax.ppermute(array, "section", [(i, target(i, peers)) for i in range(peers)])


def across_core(array, name):
    return sent(array, name, lambda i, n: i ^ CORE)


def across_first(array, name):
    return sent(array, name, lambda i, n: i ^ (Z if i & CORE else X))


def across_second(array, name):
    return sent(array, name, lambda i, n: i ^ (X if i & CORE else Z))


def from_behind(array, name):
    return sent(array, name, lambda i, n: (i + SPLIT) % n)


def after(array, *others):
    return lax.optimization_barrier((array, *others))[0]


PLACE = ((0, 1, 2, 5, 3, 4, 6, 7), (0, 1, 3, 4, 2, 5, 6, 7))


def slab_place(source, position):
    difference = source ^ position
    odd = (position & CORE) == 1
    even_place = sum(jnp.where(difference == j, PLACE[0][j], 0) for j in range(SPLIT))
    odd_place = sum(jnp.where(difference == j, PLACE[1][j], 0) for j in range(SPLIT))
    return jnp.where(odd, odd_place, even_place)


def slot_lists(phases, place, chunk, tile, cols, live, spare):
    slots = cols.shape[0]
    index = jnp.arange(slots, dtype=jnp.int32)
    count = len(phases)
    phase = jnp.full((slots,), count, jnp.int32)
    block = jnp.zeros((slots,), jnp.int32)
    for k, blocks in enumerate(phases):
        for p, c, at in blocks:
            hit = live & (place == p) & (chunk == c)
            phase = jnp.where(hit, k, phase)
            block = jnp.where(hit, at, block)
    member = phase[:, None] == jnp.arange(count, dtype=jnp.int32)[None, :]
    steps = (jnp.sum(member, axis=0, dtype=jnp.int32) + UNROLL - 1) // UNROLL
    lower = jnp.arange(count + 1)[:, None] > jnp.arange(count)[None, :]
    starts = jnp.sum(jnp.where(lower, steps[None, :], 0), axis=1, dtype=jnp.int32)
    before = (phase[None, :] == phase[:, None]) & (index[None, :] < index[:, None])
    rank = jnp.sum(before, axis=1, dtype=jnp.int32)
    base = jnp.sum(jnp.where(member, starts[None, :count] * UNROLL, 0), axis=1, dtype=jnp.int32)
    spot = jnp.where(live, base + rank, -1)
    hit = spot[None, :] == jnp.arange(slots + count * UNROLL, dtype=jnp.int32)[:, None]
    word = ((index * 32 + block) * 64 + tile) * 64 + cols
    packed = jnp.sum(jnp.where(hit, (word - spare)[None, :], 0), axis=1, dtype=jnp.int32) + spare
    return starts, packed


def phase_kernel(phase, pieces, first, columns, starts_ref, list_ref, w_ref, *refs):
    refs = list(refs)
    if not first:
        refs.pop(0)
    bias_ref = refs.pop(0) if columns else None
    piece_refs = [refs.pop(0) for _ in range(pieces)]
    acc = refs.pop(0)
    out = refs.pop(0) if columns else None
    held = refs.pop(0)
    rows = held.shape[1]
    at = 0
    for piece in piece_refs:
        for row in range(0, piece.shape[0], rows):
            held[at] = piece[row:row + rows]
            at += 1
    if first:
        acc[...] = jnp.zeros_like(acc)

    def step(it, carry):
        products = []
        places = []
        for u in range(UNROLL):
            word = list_ref[it * UNROLL + u]
            at = pl.ds(pl.multiple_of(((word >> 6) & 63) * TILE, TILE), TILE)
            x = held[(word >> 12) & 31, :, at]
            products.append(jnp.dot(x, w_ref[word >> 17], preferred_element_type=jnp.float32))
            places.append(word & 63)
        for place, product in zip(places, products):
            acc[place] = acc[place] + product
        return carry

    lax.fori_loop(starts_ref[phase], starts_ref[phase + 1], step, 0)
    for k, c in enumerate(columns):
        at = slice(c * TILE, (c + 1) * TILE)
        out[:, k * TILE:(k + 1) * TILE] = jnp.maximum(acc[c] + bias_ref[:, at], 0.0).astype(out.dtype)


def run_phase(phase, lists, weights, acc, pieces, wide, bias=None, columns=()):
    first, last = acc is None, bias is not None
    tall, piece_wide = pieces[0].shape
    slabs = sum(piece.shape[0] for piece in pieces) // tall
    smem = pl.BlockSpec(memory_space=pltpu.SMEM)
    vmem = pl.BlockSpec(memory_space=pltpu.VMEM)
    operands = [*lists, weights] + ([] if first else [acc]) + ([bias] if last else []) + list(pieces)
    shape = (wide // TILE + 1, tall, TILE)
    scratch = [pltpu.VMEM((slabs, tall, piece_wide), jnp.bfloat16)]
    out = [jax.ShapeDtypeStruct(shape, jnp.float32)]
    if last:
        out.append(jax.ShapeDtypeStruct((tall, len(columns) * TILE), jnp.bfloat16))
    aliases = {} if first else {3: 0}
    results = pl.pallas_call(
        functools.partial(phase_kernel, phase, len(pieces), first, tuple(columns)),
        out_shape=out,
        in_specs=[smem, smem] + [vmem] * (len(operands) - 2),
        out_specs=[vmem] * len(out),
        scratch_shapes=scratch,
        input_output_aliases=aliases,
        compiler_params=pltpu.CompilerParams(vmem_limit_bytes=12 << 20),
        cost_estimate=pl.CostEstimate(flops=2_000_000_000, bytes_accessed=6_000_000, transcendentals=0),
        name=f"phase_{phase}",
    )(*operands)
    return results if last else results[0]


def blocks(*slabs, columns=None):
    if columns is None:
        return tuple((place, chunk, at) for at, (place, chunk) in enumerate(slabs))
    return tuple((place, chunk, at) for at, place in enumerate(slabs) for chunk in columns)


ALL = tuple(range(CHUNKS))
FIRST_PHASES = (
    blocks(0, 1, columns=ALL),
    blocks(2, 3, 4, 5, columns=ALL),
    blocks(6, columns=ALL),
) + tuple(blocks(7, columns=(k,)) for k in ALL)
LATER_PHASES = (
    blocks((0, 0), (1, 0)),
    blocks(*((p, 0) for p in range(2, 6))),
    blocks((6, 0), (7, 0), *((p, 1) for p in range(6))),
    blocks((6, 1), (7, 1)),
)


def first_layer(own, lists, weights, bias):
    wide = own.shape[1]
    a = across_first(own, "a")
    core = across_core(own, "core")
    b = across_second(own, "b")
    acc = run_phase(0, lists, weights, None, [own, core], wide)
    a = after(a, acc)
    e = across_second(a, "e")
    pieces = [a, b, across_core(a, "ac"), across_core(b, "bc")]
    acc = run_phase(1, lists, weights, acc, pieces, wide)
    e = after(e, acc)
    pieces = [across_core(e, "ec")]
    acc = run_phase(2, lists, weights, acc, [e], wide)
    outs = []
    part = wide // TILE // CHUNKS
    for k in ALL:
        acc, out = run_phase(3 + k, lists, weights, acc, pieces, wide, bias, range(k * part, (k + 1) * part))
        outs.append(out)
    return outs


def later_layer(parts, lists, weights, bias, wide):
    done = parts[-1]
    parts = [from_behind(part, f"cross{k}") for k, part in enumerate(parts)]
    parts[0] = after(parts[0], done)
    core = [across_core(part, f"CORE{k}") for k, part in enumerate(parts[:1])]
    acc = run_phase(0, lists, weights, None, [parts[0], core[0]], wide)
    core.append(across_core(parts[1], "CORE1"))
    late = []
    for k, own in enumerate(parts):
        a = across_first(own, f"A{k}")
        b = across_second(own, f"B{k}")
        if k == 0:
            a = after(a, acc)
        e = across_second(a, f"E{k}")
        pieces = [*late, *([own, core[k]] if k else []), a, b, across_core(a, f"AC{k}"), across_core(b, f"BC{k}")]
        if k:
            e = after(e, acc)
        late = [e, across_core(e, f"EC{k}")]
        acc = run_phase(k + 1, lists, weights, acc, pieces, wide)
    return run_phase(3, lists, weights, acc, late, wide, bias, range(wide // TILE))[1]


def on_device(held, tile_values, tile_rows, tile_cols, tile_count, bias):
    position = lax.axis_index("section") % SPLIT
    own = held[0]
    wide = own.shape[1]
    tiles = wide // TILE
    live = jnp.arange(tile_rows.shape[0], dtype=jnp.int32) < tile_count[0]
    place = slab_place(tile_rows // tiles, position)
    tile = tile_rows % tiles
    part = tiles // CHUNKS
    first_lists = slot_lists(FIRST_PHASES, place, tile_cols // part, tile, tile_cols, live, tiles)
    later_lists = slot_lists(LATER_PHASES, place, tile // part, tile % part, tile_cols, live, tiles)
    bias_row = bias[None, :]
    parts = first_layer(own, first_lists, tile_values, bias_row)
    for tick in range(1, TICKS):
        slab = later_layer(parts, later_lists, tile_values, bias_row, wide)
        parts = jnp.split(slab, CHUNKS, axis=1)
    return slab[None]


def solution(mesh):
    return jax.shard_map(
        on_device,
        mesh=mesh,
        in_specs=(
            P("section", "groups", None),
            P("section", None, None),
            P("section"),
            P("section"),
            P("section"),
            P("section"),
        ),
        out_specs=P("section", "groups", None),
        check_vma=False,
    )
```

```python
import functools

import jax
import jax.numpy as jnp
from jax import lax
from jax.experimental import pallas as pl
from jax.experimental.pallas import tpu as pltpu
from jax.sharding import PartitionSpec as P

TILE = 128
SPLIT = 8
TICKS = 2
UNROLL = 32
CHUNKS = 2

CORE, X, Z = 1, 2, 4


def sent(array, name, target):
    peers = lax.axis_size("section")
    with jax.named_scope(name):
        return lax.ppermute(array, "section", [(i, target(i, peers)) for i in range(peers)])


def across_core(array, name):
    return sent(array, name, lambda i, n: i ^ CORE)


def across_first(array, name):
    return sent(array, name, lambda i, n: i ^ (Z if i & CORE else X))


def across_second(array, name):
    return sent(array, name, lambda i, n: i ^ (X if i & CORE else Z))


def from_behind(array, name):
    return sent(array, name, lambda i, n: (i + SPLIT) % n)


def after(array, *others):
    return lax.optimization_barrier((array, *others))[0]


PLACE = ((0, 1, 2, 5, 3, 4, 6, 7), (0, 1, 3, 4, 2, 5, 6, 7))


def slab_place(source, position):
    difference = source ^ position
    odd = (position & CORE) == 1
    even_place = sum(jnp.where(difference == j, PLACE[0][j], 0) for j in range(SPLIT))
    odd_place = sum(jnp.where(difference == j, PLACE[1][j], 0) for j in range(SPLIT))
    return jnp.where(odd, odd_place, even_place)


def slot_lists(phases, place, chunk, tile, cols, live, spare):
    slots = cols.shape[0]
    index = jnp.arange(slots, dtype=jnp.int32)
    count = len(phases)
    phase = jnp.full((slots,), count, jnp.int32)
    block = jnp.zeros((slots,), jnp.int32)
    for k, blocks in enumerate(phases):
        for p, c, at in blocks:
            hit = live & (place == p) & (chunk == c)
            phase = jnp.where(hit, k, phase)
            block = jnp.where(hit, at, block)
    member = phase[:, None] == jnp.arange(count, dtype=jnp.int32)[None, :]
    steps = (jnp.sum(member, axis=0, dtype=jnp.int32) + UNROLL - 1) // UNROLL
    lower = jnp.arange(count + 1)[:, None] > jnp.arange(count)[None, :]
    starts = jnp.sum(jnp.where(lower, steps[None, :], 0), axis=1, dtype=jnp.int32)
    before = (phase[None, :] == phase[:, None]) & (index[None, :] < index[:, None])
    rank = jnp.sum(before, axis=1, dtype=jnp.int32)
    base = jnp.sum(jnp.where(member, starts[None, :count] * UNROLL, 0), axis=1, dtype=jnp.int32)
    spot = jnp.where(live, base + rank, -1)
    hit = spot[None, :] == jnp.arange(slots + count * UNROLL, dtype=jnp.int32)[:, None]
    word = ((index * 32 + block) * 64 + tile) * 64 + cols
    packed = jnp.sum(jnp.where(hit, (word - spare)[None, :], 0), axis=1, dtype=jnp.int32) + spare
    return starts, packed


def phase_kernel(phase, pieces, first, columns, starts_ref, list_ref, w_ref, *refs):
    refs = list(refs)
    if not first:
        refs.pop(0)
    bias_ref = refs.pop(0) if columns else None
    piece_refs = [refs.pop(0) for _ in range(pieces)]
    acc = refs.pop(0)
    out = refs.pop(0) if columns else None
    held = refs.pop(0)
    rows = held.shape[1]
    at = 0
    for piece in piece_refs:
        for row in range(0, piece.shape[0], rows):
            held[at] = piece[row:row + rows]
            at += 1
    if first:
        acc[...] = jnp.zeros_like(acc)

    def step(it, carry):
        products = []
        places = []
        for u in range(UNROLL):
            word = list_ref[it * UNROLL + u]
            at = pl.ds(pl.multiple_of(((word >> 6) & 63) * TILE, TILE), TILE)
            x = held[(word >> 12) & 31, :, at]
            products.append(jnp.dot(x, w_ref[word >> 17], preferred_element_type=jnp.float32))
            places.append(word & 63)
        for place, product in zip(places, products):
            acc[place] = acc[place] + product
        return carry

    lax.fori_loop(starts_ref[phase], starts_ref[phase + 1], step, 0)
    for k, c in enumerate(columns):
        at = slice(c * TILE, (c + 1) * TILE)
        out[:, k * TILE:(k + 1) * TILE] = jnp.maximum(acc[c] + bias_ref[:, at], 0.0).astype(out.dtype)


def run_phase(phase, lists, weights, acc, pieces, wide, bias=None, columns=()):
    first, last = acc is None, bias is not None
    tall, piece_wide = pieces[0].shape
    slabs = sum(piece.shape[0] for piece in pieces) // tall
    smem = pl.BlockSpec(memory_space=pltpu.SMEM)
    vmem = pl.BlockSpec(memory_space=pltpu.VMEM)
    operands = [*lists, weights] + ([] if first else [acc]) + ([bias] if last else []) + list(pieces)
    shape = (wide // TILE + 1, tall, TILE)
    scratch = [pltpu.VMEM((slabs, tall, piece_wide), jnp.bfloat16)]
    out = [jax.ShapeDtypeStruct(shape, jnp.float32)]
    if last:
        out.append(jax.ShapeDtypeStruct((tall, len(columns) * TILE), jnp.bfloat16))
    aliases = {} if first else {3: 0}
    results = pl.pallas_call(
        functools.partial(phase_kernel, phase, len(pieces), first, tuple(columns)),
        out_shape=out,
        in_specs=[smem, smem] + [vmem] * (len(operands) - 2),
        out_specs=[vmem] * len(out),
        scratch_shapes=scratch,
        input_output_aliases=aliases,
        compiler_params=pltpu.CompilerParams(vmem_limit_bytes=12 << 20),
        cost_estimate=pl.CostEstimate(flops=2_000_000_000, bytes_accessed=6_000_000, transcendentals=0),
        name=f"phase_{phase}",
    )(*operands)
    return results if last else results[0]


def blocks(*slabs, columns=None):
    if columns is None:
        return tuple((place, chunk, at) for at, (place, chunk) in enumerate(slabs))
    return tuple((place, chunk, at) for at, place in enumerate(slabs) for chunk in columns)


ALL = tuple(range(CHUNKS))
FIRST_PHASES = (
    blocks(0, 1, columns=ALL),
    blocks(2, 3, 4, 5, columns=ALL),
    blocks(6, columns=ALL),
) + tuple(blocks(7, columns=(k,)) for k in ALL)
LATER_PHASES = (
    blocks((0, 0), (1, 0)),
    blocks(*((p, 0) for p in range(2, 6)), (0, 1)),
    blocks((6, 0), (7, 0), *((p, 1) for p in range(1, 6))),
    blocks((6, 1), (7, 1)),
)


def first_layer(own, lists, weights, bias):
    wide = own.shape[1]
    a = across_first(own, "a")
    core = across_core(own, "core")
    b = across_second(own, "b")
    acc = run_phase(0, lists, weights, None, [own, core], wide)
    a = after(a, acc)
    e = across_second(a, "e")
    pieces = [a, b, across_core(a, "ac"), across_core(b, "bc")]
    acc = run_phase(1, lists, weights, acc, pieces, wide)
    e = after(e, acc)
    pieces = [across_core(e, "ec")]
    acc = run_phase(2, lists, weights, acc, [e], wide)
    outs = []
    part = wide // TILE // CHUNKS
    for k in ALL:
        acc, out = run_phase(3 + k, lists, weights, acc, pieces, wide, bias, range(k * part, (k + 1) * part))
        outs.append(out)
    return outs


def later_layer(parts, lists, weights, bias, wide):
    done = parts[-1]
    parts = [from_behind(part, f"cross{k}") for k, part in enumerate(parts)]
    parts[0] = after(parts[0], done)
    core = [across_core(part, f"CORE{k}") for k, part in enumerate(parts[:1])]
    acc = run_phase(0, lists, weights, None, [parts[0], core[0]], wide)
    core.append(across_core(parts[1], "CORE1"))
    late = []
    for k, own in enumerate(parts):
        a = across_first(own, f"A{k}")
        b = across_second(own, f"B{k}")
        if k == 0:
            a = after(a, acc)
        e = across_second(a, f"E{k}")
        pieces = [*late, *core[1:1 + k], a, b, across_core(a, f"AC{k}"), across_core(b, f"BC{k}")]
        if k == 0:
            pieces.append(parts[1])
        if k:
            e = after(e, acc)
        late = [e, across_core(e, f"EC{k}")]
        acc = run_phase(k + 1, lists, weights, acc, pieces, wide)
    return run_phase(3, lists, weights, acc, late, wide, bias, range(wide // TILE))[1]


def on_device(held, tile_values, tile_rows, tile_cols, tile_count, bias):
    position = lax.axis_index("section") % SPLIT
    own = held[0]
    wide = own.shape[1]
    tiles = wide // TILE
    live = jnp.arange(tile_rows.shape[0], dtype=jnp.int32) < tile_count[0]
    place = slab_place(tile_rows // tiles, position)
    tile = tile_rows % tiles
    part = tiles // CHUNKS
    first_lists = slot_lists(FIRST_PHASES, place, tile_cols // part, tile, tile_cols, live, tiles)
    later_lists = slot_lists(LATER_PHASES, place, tile // part, tile % part, tile_cols, live, tiles)
    bias_row = bias[None, :]
    parts = first_layer(own, first_lists, tile_values, bias_row)
    for tick in range(1, TICKS):
        slab = later_layer(parts, later_lists, tile_values, bias_row, wide)
        parts = jnp.split(slab, CHUNKS, axis=1)
    return slab[None]


def solution(mesh):
    return jax.shard_map(
        on_device,
        mesh=mesh,
        in_specs=(
            P("section", "groups", None),
            P("section", None, None),
            P("section"),
            P("section"),
            P("section"),
            P("section"),
        ),
        out_specs=P("section", "groups", None),
        check_vma=False,
    )
```
